32 devices in a mesh: grp: 2 (over y), tm: 4 (over z), tmpl: 2 (over x), chan: 2 (over core).
Axes of the slice: x: 2, y: 2, z: 4, core: 2. Of those that a mesh axis runs over, the one named last changes fastest.
Arguments:
- record: bfloat16 [32, 4096], P('chan', ('grp', 'tm')), parts along dimension 1, may hold values from -640 to 640
- templates: bfloat16 [2, 768, 32, 512], P('tmpl', 'tm', 'chan'), may hold values from -0.046875 to 0.046875
- span_list: int32 [8, 4], P(('grp', 'tm')), parts along dimension 0, may hold values from -1 to 3, as said below
Outputs:
- scan_out: float32 [1536, 4096], P(('tmpl', 'chan'), ('grp', 'tm')), parts along dimension 1
The draws below stay inside these ranges and needn't reach their ends.
There are 2 independent parts, one for each index of `grp`. The reference program is written for one: setup_inputs(seed, part) draws one part's arguments, and reference() takes and returns one part's arrays. A program takes and returns all parts, laid end to end along the dimension named above; an argument that names none is the same for every part. Nothing has to cross between parts.
Inputs may be any that keep to these rules, and one draw needn't show every extreme that they name: `span_list`: each shard lists distinct blocks in its first slots and -1 in the rest; between 1 and 4 blocks a shard, exactly 8 in all shards together, and some shard lists 4.
All inputs are finite; a program needn't handle non-finite values.
Results may differ from the reference program's by a relative error of at most 0.0003.
Values may be sent and summed in bfloat16 or wider, within the bound.
A program may use at most 64 MiB of HBM per device.

```python
import math
import jax
import jax.numpy as jnp
import numpy as np
from jax import lax

C = 32
L = 512
K = 1536
SPAN = 128
NCH_DEV = 4
MOST_DENSE = 4
TIME = 2048
KG = 768
DENSE_TOTAL = 8
N_TM = 4
N_TMPL = 2


def draw_record(key, part):
    keys = jax.random.split(jax.random.fold_in(key, 11), 3)
    blocks = TIME // 8
    spread = math.log(10.0)
    base = jax.random.truncated_normal(keys[0], -4.0, 4.0, (C, TIME), jnp.float32)
    chan_scale = jnp.exp(jax.random.uniform(keys[1], (C, 1), jnp.float32, 0.0, spread))
    time_scale = jnp.exp(jax.random.uniform(keys[2], (1, blocks), jnp.float32, 0.0, spread))
    time_scale = jnp.repeat(time_scale, 8, axis=1)
    return (base * chan_scale * time_scale).astype(jnp.bfloat16)


def draw_span_list(key, part):
    keys = jax.random.split(jax.random.fold_in(key, 23), N_TM + 1)
    pattern = np.zeros(N_TM, np.int32)
    pattern[0] = 2
    pattern[1] = -1
    pattern[2] = -1
    for place in range(3, N_TM):
        if place % 2 == 1 and place + 1 < N_TM:
            pattern[place] = 1
        elif place % 2 == 0:
            pattern[place] = -1
    order = jax.random.permutation(keys[0], N_TM)
    counts = jnp.zeros((N_TM,), jnp.int32).at[order].set(jnp.asarray(pattern + 2, jnp.int32))
    picks = jax.vmap(lambda sub: jax.random.permutation(sub, NCH_DEV)[:MOST_DENSE])(keys[1:])
    column = jnp.arange(MOST_DENSE, dtype=jnp.int32)[None, :]
    return jnp.where(column < counts[:, None], picks.astype(jnp.int32), -1).astype(jnp.int32)


def block_scale(rng, extent, shards, low, largest):
    level = 1.0
    for position, blocks in shards:
        heights = jax.random.uniform(jax.random.fold_in(jax.random.fold_in(rng, 6), position), (blocks,), jnp.float32, low / len(shards), largest / len(shards))
        level = level * jnp.repeat(jnp.exp(heights), extent[position] // blocks).reshape((-1,) + (1,) * (len(extent) - 1 - position))
    return level


def scatter_about(key, dims, scale, bound, pieces=(), kind=jnp.bfloat16):
    drawn = scale * jax.random.normal(key, dims, jnp.float32)
    if pieces:
        drawn = drawn * block_scale(key, dims, pieces, -0.22, 0.18)
    return jnp.clip(drawn, -bound, bound).astype(kind)


def setup_inputs(seed: int = 0, part: int = 0) -> dict:
    key_of = jax.random.split(jax.random.key(seed), 4)
    part_splits = jax.random.split(jax.random.fold_in(key_of[3], part), 4)
    return {
        "record": draw_record(jax.random.fold_in(jax.random.fold_in(key_of[3], part), 71), part),
        "templates": scatter_about(key_of[1], (N_TMPL, KG, C, L), (C * L) ** -0.5, 0.046875, ((0, 2), (1, 4), (2, 2))),
        "span_list": draw_span_list(jax.random.fold_in(jax.random.fold_in(key_of[3], part), 71), part),
    }


def windows(segment):
    seg_len = segment.shape[1]
    tiled = jnp.tile(segment, (1, SPAN + 1))
    flattened = tiled[:, :SPAN * (seg_len + 1)]
    return flattened.reshape(segment.shape[0], SPAN, seg_len + 1)[:, :, :L]

def reference(record, templates, span_list):
    shard_len = NCH_DEV * SPAN
    padded = jnp.concatenate([record, jnp.zeros((C, shard_len), record.dtype)], axis=1)
    flat_tmpl = templates.reshape(K, C * L)
    listed = span_list.reshape(-1).astype(jnp.int32)
    usable = (listed >= 0).astype(jnp.int32)
    chosen = jnp.argsort(1 - usable, stable=True)[:DENSE_TOTAL].astype(jnp.int32)

    def one_slot(slot_index):
        span_at = listed[slot_index]
        sample_start = (slot_index // MOST_DENSE * shard_len + span_at * SPAN).astype(jnp.int32)
        segment = lax.dynamic_slice_in_dim(padded, sample_start, SPAN + L, 1)
        window_set = windows(segment)
        columns = window_set.transpose(0, 2, 1).reshape(C * L, SPAN)
        correlation = jnp.dot(flat_tmpl, columns, preferred_element_type=jnp.float32)
        energy = lax.optimization_barrier(jnp.sum(jnp.square(window_set.astype(jnp.float32)), axis=(0, 2)))
        return correlation * lax.rsqrt(energy / (C * L) + 1e-05)[None, :]
    results = lax.map(one_slot, chosen)
    scattered = jnp.zeros((N_TM * MOST_DENSE, K, SPAN), jnp.float32).at[chosen].set(results)
    return scattered.transpose(1, 0, 2).reshape(K, N_TM * MOST_DENSE * SPAN)
```

```python
import functools

import jax
import jax.numpy as jnp
from jax import lax
from jax.experimental import pallas as pl
from jax.experimental.pallas import tpu as pltpu
from jax.sharding import PartitionSpec as P

SPAN = 128
CODES = 32767.0
MESH = pl.DeviceIdType.MESH


def kernel(n, rows, chans, slots, span_ref, rec_ref, lhs_ref, out_ref, rec_all, shifted, hankel, acc, sib, codes, scales,
           codes_in, scales_in, e_mine, e_sib, rec_send, rec_recv, sib_send, sib_recv, code_send, code_recv,
           scale_send, scale_recv, e_send, e_recv):
    z = lax.axis_index("tm")
    core = lax.axis_index("chan")
    half = n // 2
    home = z // half
    own_part = z % half
    other = {"tm": z, "chan": 1 - core}
    blocks = n * slots

    barrier = pltpu.get_barrier_semaphore()

    def greet(i, _):
        peer = lax.rem(z + i // 2, n)
        to = lax.rem(core + i % 2, 2)
        pl.semaphore_signal(barrier, inc=1, device_id={"tm": peer, "chan": to}, device_id_type=MESH)
        return 0

    lax.fori_loop(1, 2 * n, greet, 0)
    rec_all[z] = rec_ref[...]
    rec_all[n] = jnp.zeros_like(rec_ref)
    acc[...] = jnp.zeros_like(acc)
    pl.semaphore_wait(barrier, 2 * n - 1)

    def record_copy(i):
        peer = lax.rem(z + i, n)
        return pltpu.make_async_remote_copy(
            src_ref=rec_ref, dst_ref=rec_all.at[z], send_sem=rec_send.at[peer], recv_sem=rec_recv.at[z],
            device_id={"tm": peer, "chan": core}, device_id_type=MESH)

    def record_arrival(i):
        peer = lax.rem(z + i, n)
        return pltpu.make_async_remote_copy(
            src_ref=rec_ref, dst_ref=rec_all.at[peer], send_sem=rec_send.at[peer], recv_sem=rec_recv.at[peer],
            device_id={"tm": peer, "chan": core}, device_id_type=MESH)

    lax.fori_loop(1, n, lambda i, _: (record_copy(i).start(), 0)[1], 0)
    lax.fori_loop(1, n, lambda i, _: (record_arrival(i).wait_recv(), 0)[1], 0)

    for part in range(2):
        for b in range(slots):
            piece = rec_all[z + part, :, b * SPAN:(b + 1) * SPAN].astype(jnp.float32)
            e_mine[part * slots + b:part * slots + b + 1, :] = jnp.sum(piece * piece, axis=0, keepdims=True)
    energy_copy = pltpu.make_async_remote_copy(
        src_ref=e_mine, dst_ref=e_sib, send_sem=e_send, recv_sem=e_recv, device_id=other, device_id_type=MESH)
    energy_copy.start()

    row = lax.broadcasted_iota(jnp.int32, (chans, 8, SPAN), 1)
    lane = lax.broadcasted_iota(jnp.int32, (chans, 8, SPAN), 2)

    def spread(x):
        return jnp.broadcast_to(x.astype(jnp.float32)[:, None, :], (chans, 8, SPAN))

    def shift_rows(s, _):
        for b in range(slots):
            now = spread(rec_all[s, :, b * SPAN:(b + 1) * SPAN])
            if b + 1 < slots:
                after = spread(rec_all[s, :, (b + 1) * SPAN:(b + 2) * SPAN])
            else:
                after = spread(rec_all[s + 1, :, :SPAN])
            y = jnp.where(lane >= row, now, after)
            for bit in (1, 2, 4):
                y = jnp.where((row & bit) > 0, pltpu.roll(y, SPAN - bit, 2), y)
            shifted[s * slots + b] = y
        return 0

    lax.fori_loop(0, n, shift_rows, 0)
    shifted[blocks] = jnp.zeros((chans, 8, SPAN), jnp.float32)

    def build(pair):
        for par in range(2):
            now = shifted[2 * pair + par]
            after = shifted[2 * pair + par + 1]
            for a in range(0, SPAN // 8, 2):
                both = []
                for d in (a, a + 1):
                    y = now
                    if d > 0:
                        y = pltpu.roll(jnp.where(lane >= 8 * d, now, after), SPAN - 8 * d, 2)
                    both.append(y)
                hankel[:, 8 * a:8 * a + 16, par * SPAN:(par + 1) * SPAN] = jnp.concatenate(both, axis=1).astype(jnp.bfloat16)

    def multiply(pair):
        build(pair)
        product = jnp.dot(lhs_ref[...], hankel[...].reshape(chans * SPAN, 2 * SPAN), preferred_element_type=jnp.float32)
        for par in range(2):
            for j in range(4):
                at = 2 * pair + par - j + 3
                acc[at] += product[j * rows:(j + 1) * rows, par * SPAN:(par + 1) * SPAN]

    def sibling_copy(dest):
        return pltpu.make_async_remote_copy(
            src_ref=acc.at[pl.ds(3 + slots * dest + 2 * (1 - core), 2)], dst_ref=sib.at[dest],
            send_sem=sib_send.at[dest], recv_sem=sib_recv.at[dest], device_id=other, device_id_type=MESH)

    def result_copies(dest, part, from_core):
        to = {"tm": dest, "chan": home}
        slot = part * 2 + from_core
        return (
            pltpu.make_async_remote_copy(
                src_ref=codes.at[dest], dst_ref=codes_in.at[part, pl.ds(2 * from_core, 2)], send_sem=code_send.at[dest],
                recv_sem=code_recv.at[slot], device_id=to, device_id_type=MESH),
            pltpu.make_async_remote_copy(
                src_ref=scales.at[dest], dst_ref=scales_in.at[part, pl.ds(2 * from_core, 2)], send_sem=scale_send.at[dest],
                recv_sem=scale_recv.at[slot], device_id=to, device_id_type=MESH),
        )

    def finish(dest):
        sibling_copy(dest).wait_recv()
        keep = jnp.logical_and(dest == z, core == home)
        for b in range(2):
            total = acc[3 + slots * dest + 2 * core + b] + sib[dest, b]
            top = jnp.maximum(jnp.max(jnp.abs(total), axis=0, keepdims=True), 1e-37)
            coded = jnp.round((total * (1.0 / top)) * CODES).astype(jnp.int32).astype(jnp.int16)
            scale = jnp.broadcast_to(top * (1.0 / CODES), (8, SPAN))

            @pl.when(keep)
            def _():
                codes_in[own_part, 2 * core + b] = coded
                scales_in[own_part, 2 * core + b] = scale

            @pl.when(jnp.logical_not(keep))
            def _():
                codes[dest, b] = coded
                scales[dest, b] = scale

        @pl.when(jnp.logical_not(keep))
        def _():
            for copy in result_copies(dest, own_part, core):
                copy.start()

    def step(d, _):
        dest = n - 1 - d
        multiply(2 * dest + 1)
        multiply(2 * dest)
        sibling_copy(dest).start()

        @pl.when(d > 0)
        def _():
            finish(dest + 1)

        return 0

    lax.fori_loop(0, n, step, 0)
    finish(0)

    energy_copy.wait()
    e = e_mine[...] + e_sib[...]
    i0 = lax.broadcasted_iota(jnp.int32, (SPAN, SPAN), 0)
    i1 = lax.broadcasted_iota(jnp.int32, (SPAN, SPAN), 1)
    dot = functools.partial(jnp.dot, preferred_element_type=jnp.float32, precision=lax.Precision.HIGHEST)
    tails = dot(e, jnp.where(i0 >= i1, 1.0, 0.0))
    heads = dot(e, jnp.where(i0 < i1, 1.0, 0.0))
    sums = jnp.sum(e, axis=1, keepdims=True)
    for b in range(slots):
        energy = tails[b:b + 1] + heads[b + 4:b + 5] + sums[b + 1:b + 2] + sums[b + 2:b + 3] + sums[b + 3:b + 4]
        e_mine[b:b + 1, :] = lax.rsqrt(energy / (2 * chans * 4 * SPAN) + 1e-05)

    def arrival(i, _):
        part, from_core = i // 2, i % 2
        source = core * half + part

        @pl.when(jnp.logical_not(jnp.logical_and(source == z, from_core == core)))
        def _():
            for copy in result_copies(0, part, from_core):
                copy.wait_recv()

        return 0

    lax.fori_loop(0, n, arrival, 0)

    for slot in range(slots):
        at = span_ref[0, slot]
        block = jnp.maximum(at, 0)
        inverse = jnp.where(at >= 0, e_mine[pl.ds(block, 1), :], 0.0)
        for part in range(half):
            values = codes_in[part, block].astype(jnp.int32).astype(jnp.float32)
            scale = scales_in[part, block, 0:1] * inverse
            out_ref[part * rows:(part + 1) * rows, slot * SPAN:(slot + 1) * SPAN] = values * scale

    def drain(dest, _):
        sibling_copy(dest).wait_send()

        @pl.when(jnp.logical_not(jnp.logical_and(dest == z, core == home)))
        def _():
            for copy in result_copies(dest, own_part, core):
                copy.wait_send()

        @pl.when(dest != z)
        def _():
            pltpu.make_async_remote_copy(
                src_ref=rec_ref, dst_ref=rec_all.at[z], send_sem=rec_send.at[dest], recv_sem=rec_recv.at[z],
                device_id={"tm": dest, "chan": core}, device_id_type=MESH).wait_send()

        return 0

    lax.fori_loop(0, n, drain, 0)


def local(n, record, templates, span_list):
    _, rows, chans, length = templates.shape
    slots = span_list.shape[1]
    blocks = n * slots
    lhs = templates[0].reshape(rows, chans, length // SPAN, SPAN).transpose(2, 0, 1, 3).reshape(4 * rows, chans * SPAN)
    vmem = pl.BlockSpec(memory_space=pltpu.VMEM)
    dma = pltpu.SemaphoreType.DMA
    return pl.pallas_call(
        functools.partial(kernel, n, rows, chans, slots),
        out_shape=jax.ShapeDtypeStruct((rows * n // 2, slots * SPAN), jnp.float32),
        in_specs=[pl.BlockSpec(memory_space=pltpu.SMEM), vmem, vmem],
        out_specs=vmem,
        scratch_shapes=[
            pltpu.VMEM((n + 1, chans, record.shape[1]), jnp.bfloat16),
            pltpu.VMEM((blocks + 1, chans, 8, SPAN), jnp.float32),
            pltpu.VMEM((chans, SPAN, 2 * SPAN), jnp.bfloat16),
            pltpu.VMEM((blocks + 3, rows, SPAN), jnp.float32),
            pltpu.VMEM((n, 2, rows, SPAN), jnp.float32),
            pltpu.VMEM((n, 2, rows, SPAN), jnp.int16),
            pltpu.VMEM((n, 2, 8, SPAN), jnp.float32),
            pltpu.VMEM((n // 2, 4, rows, SPAN), jnp.int16),
            pltpu.VMEM((n // 2, 4, 8, SPAN), jnp.float32),
            pltpu.VMEM((8, SPAN), jnp.float32),
            pltpu.VMEM((8, SPAN), jnp.float32),
            dma((n,)), dma((n,)), dma((n,)), dma((n,)), dma((n,)), dma((n,)), dma((n,)), dma((n,)),
            dma, dma,
        ],
        compiler_params=pltpu.CompilerParams(collective_id=0, has_side_effects=True, vmem_limit_bytes=50 * 2**20),
    )(span_list, record, lhs)


def solution(mesh):
    in_specs = (P("chan", ("grp", "tm")), P("tmpl", "tm", "chan", None), P(("grp", "tm"), None))
    out_specs = P(("tmpl", "chan"), ("grp", "tm"))
    return jax.shard_map(functools.partial(local, mesh.shape["tm"]), mesh=mesh, in_specs=in_specs, out_specs=out_specs, check_vma=False)
```

```python
import functools

import jax
import jax.numpy as jnp
from jax import lax
from jax.experimental import pallas as pl
from jax.experimental.pallas import tpu as pltpu
from jax.sharding import PartitionSpec as P

SPAN = 128
CODES = 32767.0
MESH = pl.DeviceIdType.MESH


def kernel(n, rows, chans, slots, span_ref, rec_ref, tmpl_ref, out_ref, tmpl, lhs, rec_all, shifted, hankel_a, hankel_b, acc, sib, codes, scales,
           codes_in, scales_in, e_mine, e_sib, rec_send, rec_recv, sib_send, sib_recv, code_send, code_recv,
           scale_send, scale_recv, e_send, e_recv, tmpl_sem):
    z = lax.axis_index("tm")
    core = lax.axis_index("chan")
    half = n // 2
    home = z // half
    own_part = z % half
    other = {"tm": z, "chan": 1 - core}
    blocks = n * slots

    tmpl_copy = pltpu.make_async_copy(tmpl_ref.at[0], tmpl, tmpl_sem)
    tmpl_copy.start()
    barrier = pltpu.get_barrier_semaphore()

    def greet(i, _):
        peer = lax.rem(z + i // 2, n)
        to = lax.rem(core + i % 2, 2)
        pl.semaphore_signal(barrier, inc=1, device_id={"tm": peer, "chan": to}, device_id_type=MESH)
        return 0

    lax.fori_loop(1, 2 * n, greet, 0)
    rec_all[z] = rec_ref[...]
    rec_all[n] = jnp.zeros_like(rec_ref)
    acc[...] = jnp.zeros_like(acc)
    pl.semaphore_wait(barrier, 2 * n - 1)

    def record_copy(i):
        peer = lax.rem(z + i, n)
        return pltpu.make_async_remote_copy(
            src_ref=rec_ref, dst_ref=rec_all.at[z], send_sem=rec_send.at[peer], recv_sem=rec_recv.at[z],
            device_id={"tm": peer, "chan": core}, device_id_type=MESH)

    def record_arrival(i):
        peer = lax.rem(z + i, n)
        return pltpu.make_async_remote_copy(
            src_ref=rec_ref, dst_ref=rec_all.at[peer], send_sem=rec_send.at[peer], recv_sem=rec_recv.at[peer],
            device_id={"tm": peer, "chan": core}, device_id_type=MESH)

    lax.fori_loop(1, n, lambda i, _: (record_copy(i).start(), 0)[1], 0)

    tmpl_copy.wait()
    group = 16 if rows % 16 == 0 else 8

    def arrange(g, _):
        for j in range(4):
            turned = jnp.swapaxes(tmpl[pl.ds(g * group, group), :, j * SPAN:(j + 1) * SPAN], 0, 1)
            at = pl.multiple_of(j * rows + g * group, group)
            for c in range(chans):
                lhs[pl.ds(at, group), c * SPAN:(c + 1) * SPAN] = turned[c]
        return 0

    lax.fori_loop(0, rows // group, arrange, 0)
    lax.fori_loop(1, n, lambda i, _: (record_arrival(i).wait_recv(), 0)[1], 0)

    for part in range(2):
        for b in range(slots):
            piece = rec_all[z + part, :, b * SPAN:(b + 1) * SPAN].astype(jnp.float32)
            e_mine[part * slots + b:part * slots + b + 1, :] = jnp.sum(piece * piece, axis=0, keepdims=True)
    energy_copy = pltpu.make_async_remote_copy(
        src_ref=e_mine, dst_ref=e_sib, send_sem=e_send, recv_sem=e_recv, device_id=other, device_id_type=MESH)
    energy_copy.start()

    row = lax.broadcasted_iota(jnp.int32, (chans, 8, SPAN), 1)
    lane = lax.broadcasted_iota(jnp.int32, (chans, 8, SPAN), 2)

    def spread(x):
        return jnp.broadcast_to(x.astype(jnp.float32)[:, None, :], (chans, 8, SPAN))

    def shift_rows(s, _):
        for b in range(slots):
            now = spread(rec_all[s, :, b * SPAN:(b + 1) * SPAN])
            if b + 1 < slots:
                after = spread(rec_all[s, :, (b + 1) * SPAN:(b + 2) * SPAN])
            else:
                after = spread(rec_all[s + 1, :, :SPAN])
            y = jnp.where(lane >= row, now, after)
            for bit in (1, 2, 4):
                y = jnp.where((row & bit) > 0, pltpu.roll(y, SPAN - bit, 2), y)
            shifted[s * slots + b] = y
        return 0

    lax.fori_loop(0, n, shift_rows, 0)
    shifted[blocks] = jnp.zeros((chans, 8, SPAN), jnp.float32)

    def build(pair, hankel):
        for par in range(2):
            now = shifted[2 * pair + par]
            after = shifted[2 * pair + par + 1]
            for a in range(0, SPAN // 8, 2):
                both = []
                for d in (a, a + 1):
                    y = now
                    if d > 0:
                        y = pltpu.roll(jnp.where(lane >= 8 * d, now, after), SPAN - 8 * d, 2)
                    both.append(y)
                hankel[:, 8 * a:8 * a + 16, par * SPAN:(par + 1) * SPAN] = jnp.concatenate(both, axis=1).astype(jnp.bfloat16)

    def multiply(pair, hankel):
        product = jnp.dot(lhs[...], hankel[...].reshape(chans * SPAN, 2 * SPAN), preferred_element_type=jnp.float32)
        for par in range(2):
            for j in range(4):
                at = 2 * pair + par - j + 3
                acc[at] += product[j * rows:(j + 1) * rows, par * SPAN:(par + 1) * SPAN]

    rising = jnp.where(z >= half, 1, 0)

    def pair_at(t):
        return rising * t + (1 - rising) * (2 * n - 1 - t)

    def chunk_at(t):
        return pair_at(t) - 2 * rising

    def sibling_copy(u):
        return pltpu.make_async_remote_copy(
            src_ref=acc.at[pl.ds(3 + 2 * u, 2)], dst_ref=sib.at[u],
            send_sem=sib_send.at[u], recv_sem=sib_recv.at[u], device_id=other, device_id_type=MESH)

    def result_copies(u, part):
        to = {"tm": u // 2, "chan": home}
        slot = part * 2 + u % 2
        return (
            pltpu.make_async_remote_copy(
                src_ref=codes.at[u], dst_ref=codes_in.at[part, pl.ds(2 * (u % 2), 2)], send_sem=code_send.at[u],
                recv_sem=code_recv.at[slot], device_id=to, device_id_type=MESH),
            pltpu.make_async_remote_copy(
                src_ref=scales.at[u], dst_ref=scales_in.at[part, pl.ds(2 * (u % 2), 2)], send_sem=scale_send.at[u],
                recv_sem=scale_recv.at[slot], device_id=to, device_id_type=MESH),
        )

    def hand_over(u):
        @pl.when(jnp.logical_and(jnp.logical_and(u >= 0, u < 2 * n), lax.rem(u + 2, 2) != core))
        def _():
            sibling_copy(u).start()

    def finish(u):
        @pl.when(jnp.logical_and(jnp.logical_and(u >= 0, u < 2 * n), lax.rem(u + 2, 2) == core))
        def _():
            sibling_copy(u).wait_recv()
            keep = jnp.logical_and(u // 2 == z, core == home)
            for b in range(2):
                total = acc[3 + 2 * u + b] + sib[u, b]
                top = jnp.maximum(jnp.max(jnp.abs(total), axis=0, keepdims=True), 1e-37)
                coded = jnp.round((total * (1.0 / top)) * CODES).astype(jnp.int32).astype(jnp.int16)
                scale = jnp.broadcast_to(top * (1.0 / CODES), (8, SPAN))

                @pl.when(keep)
                def _():
                    codes_in[own_part, 2 * core + b] = coded
                    scales_in[own_part, 2 * core + b] = scale

                @pl.when(jnp.logical_not(keep))
                def _():
                    codes[u, b] = coded
                    scales[u, b] = scale

            @pl.when(jnp.logical_not(keep))
            def _():
                for copy in result_copies(u, own_part):
                    copy.start()

    build(pair_at(0), hankel_a)

    def step(i, _):
        t = 2 * i
        build(pair_at(t + 1), hankel_b)
        multiply(pair_at(t), hankel_a)
        hand_over(chunk_at(t))
        finish(chunk_at(t - 1))
        build(jnp.clip(pair_at(t + 2), 0, 2 * n - 1), hankel_a)
        multiply(pair_at(t + 1), hankel_b)
        hand_over(chunk_at(t + 1))
        finish(chunk_at(t))
        return 0

    lax.fori_loop(0, n, step, 0)
    hand_over(chunk_at(2 * n))
    hand_over(chunk_at(2 * n + 1))
    finish(chunk_at(2 * n - 1))
    finish(chunk_at(2 * n))
    finish(chunk_at(2 * n + 1))

    energy_copy.wait()
    e = e_mine[...] + e_sib[...]
    i0 = lax.broadcasted_iota(jnp.int32, (SPAN, SPAN), 0)
    i1 = lax.broadcasted_iota(jnp.int32, (SPAN, SPAN), 1)
    dot = functools.partial(jnp.dot, preferred_element_type=jnp.float32, precision=lax.Precision.HIGHEST)
    tails = dot(e, jnp.where(i0 >= i1, 1.0, 0.0))
    heads = dot(e, jnp.where(i0 < i1, 1.0, 0.0))
    sums = jnp.sum(e, axis=1, keepdims=True)
    for b in range(slots):
        energy = tails[b:b + 1] + heads[b + 4:b + 5] + sums[b + 1:b + 2] + sums[b + 2:b + 3] + sums[b + 3:b + 4]
        e_mine[b:b + 1, :] = lax.rsqrt(energy / (2 * chans * 4 * SPAN) + 1e-05)

    def arrival(i, _):
        part, from_core = i // 2, i % 2
        source = core * half + part

        @pl.when(jnp.logical_not(jnp.logical_and(source == z, from_core == core)))
        def _():
            for copy in result_copies(from_core, part):
                copy.wait_recv()

        return 0

    lax.fori_loop(0, n, arrival, 0)

    for slot in range(slots):
        at = span_ref[0, slot]
        block = jnp.maximum(at, 0)
        inverse = jnp.where(at >= 0, e_mine[pl.ds(block, 1), :], 0.0)
        for part in range(half):
            values = codes_in[part, block].astype(jnp.int32).astype(jnp.float32)
            scale = scales_in[part, block, 0:1] * inverse
            out_ref[part * rows:(part + 1) * rows, slot * SPAN:(slot + 1) * SPAN] = values * scale

    def drain(u, _):
        mine = u % 2 == core

        @pl.when(jnp.logical_not(mine))
        def _():
            sibling_copy(u).wait_send()

        @pl.when(jnp.logical_and(mine, jnp.logical_not(jnp.logical_and(u // 2 == z, core == home))))
        def _():
            for copy in result_copies(u, own_part):
                copy.wait_send()

        return 0

    lax.fori_loop(0, 2 * n, drain, 0)
    lax.fori_loop(1, n, lambda i, _: (record_copy(i).wait_send(), 0)[1], 0)


def local(n, record, templates, span_list):
    _, rows, chans, _ = templates.shape
    slots = span_list.shape[1]
    blocks = n * slots
    vmem = pl.BlockSpec(memory_space=pltpu.VMEM)
    dma = pltpu.SemaphoreType.DMA
    return pl.pallas_call(
        functools.partial(kernel, n, rows, chans, slots),
        out_shape=jax.ShapeDtypeStruct((rows * n // 2, slots * SPAN), jnp.float32),
        in_specs=[pl.BlockSpec(memory_space=pltpu.SMEM), vmem, pl.BlockSpec(memory_space=pltpu.HBM)],
        out_specs=vmem,
        scratch_shapes=[
            pltpu.VMEM(templates.shape[1:], jnp.bfloat16),
            pltpu.VMEM((4 * rows, chans * SPAN), jnp.bfloat16),
            pltpu.VMEM((n + 1, chans, record.shape[1]), jnp.bfloat16),
            pltpu.VMEM((blocks + 1, chans, 8, SPAN), jnp.float32),
            pltpu.VMEM((chans, SPAN, 2 * SPAN), jnp.bfloat16),
            pltpu.VMEM((chans, SPAN, 2 * SPAN), jnp.bfloat16),
            pltpu.VMEM((blocks + 3, rows, SPAN), jnp.float32),
            pltpu.VMEM((2 * n, 2, rows, SPAN), jnp.float32),
            pltpu.VMEM((2 * n, 2, rows, SPAN), jnp.int16),
            pltpu.VMEM((2 * n, 2, 8, SPAN), jnp.float32),
            pltpu.VMEM((n // 2, 4, rows, SPAN), jnp.int16),
            pltpu.VMEM((n // 2, 4, 8, SPAN), jnp.float32),
            pltpu.VMEM((8, SPAN), jnp.float32),
            pltpu.VMEM((8, SPAN), jnp.float32),
            dma((n,)), dma((n,)), dma((2 * n,)), dma((2 * n,)), dma((2 * n,)), dma((n,)), dma((2 * n,)), dma((n,)),
            dma, dma, dma,
        ],
        compiler_params=pltpu.CompilerParams(collective_id=0, has_side_effects=True, vmem_limit_bytes=62 * 2**20),
    )(span_list, record, templates)


def solution(mesh):
    in_specs = (P("chan", ("grp", "tm")), P("tmpl", "tm", "chan", None), P(("grp", "tm"), None))
    out_specs = P(("tmpl", "chan"), ("grp", "tm"))
    return jax.shard_map(functools.partial(local, mesh.shape["tm"]), mesh=mesh, in_specs=in_specs, out_specs=out_specs, check_vma=False)
```

```python
import functools

import jax
import jax.numpy as jnp
from jax import lax
from jax.experimental import pallas as pl
from jax.experimental.pallas import tpu as pltpu
from jax.sharding import PartitionSpec as P

SPAN = 128
CODES = 32767.0
MESH = pl.DeviceIdType.MESH


def kernel(n, rows, chans, slots, span_ref, rec_ref, tmpl_ref, out_ref, tmpl, lhs, rec_all, ring_a, ring_b, ring_c, ring_d, acc, sib, codes, scales,
           codes_in, scales_in, e_mine, e_sib, rec_send, rec_recv, sib_send, sib_recv, code_send, code_recv,
           scale_send, scale_recv, e_send, e_recv, tmpl_sem):
    z = lax.axis_index("tm")
    core = lax.axis_index("chan")
    half = n // 2
    home = z // half
    own_part = z % half
    other = {"tm": z, "chan": 1 - core}
    ring = (ring_a, ring_b, ring_c, ring_d)

    tmpl_copy = pltpu.make_async_copy(tmpl_ref.at[0], tmpl, tmpl_sem)
    tmpl_copy.start()
    barrier = pltpu.get_barrier_semaphore()

    def greet(i, _):
        peer = lax.rem(z + i // 2, n)
        to = lax.rem(core + i % 2, 2)
        pl.semaphore_signal(barrier, inc=1, device_id={"tm": peer, "chan": to}, device_id_type=MESH)
        return 0

    lax.fori_loop(1, 2 * n, greet, 0)
    rec_all[z] = rec_ref[...]
    rec_all[n] = jnp.zeros_like(rec_ref)
    rec_all[n + 1] = jnp.zeros_like(rec_ref)
    tmpl_copy.wait()
    group = 16 if rows % 16 == 0 else 8

    def arrange(g, _):
        for j in range(4):
            turned = jnp.swapaxes(tmpl[pl.ds(g * group, group), :, j * SPAN:(j + 1) * SPAN], 0, 1)
            at = pl.multiple_of(j * rows + g * group, group)
            for c in range(chans):
                lhs[pl.ds(at, group), c * SPAN:(c + 1) * SPAN] = turned[c]
        return 0

    pl.semaphore_wait(barrier, 2 * n - 1)

    def record_copy(i):
        peer = lax.rem(z + i, n)
        return pltpu.make_async_remote_copy(
            src_ref=rec_ref, dst_ref=rec_all.at[z], send_sem=rec_send.at[peer], recv_sem=rec_recv.at[z],
            device_id={"tm": peer, "chan": core}, device_id_type=MESH)

    def record_arrival(i):
        peer = lax.rem(z + i, n)
        return pltpu.make_async_remote_copy(
            src_ref=rec_ref, dst_ref=rec_all.at[peer], send_sem=rec_send.at[peer], recv_sem=rec_recv.at[peer],
            device_id={"tm": peer, "chan": core}, device_id_type=MESH)

    lax.fori_loop(1, n, lambda i, _: (record_copy(i).start(), 0)[1], 0)

    lax.fori_loop(0, rows // group, arrange, 0)
    lax.fori_loop(1, n, lambda i, _: (record_arrival(i).wait_recv(), 0)[1], 0)

    for part in range(2):
        for b in range(slots):
            piece = rec_all[z + part, :, b * SPAN:(b + 1) * SPAN].astype(jnp.float32)
            e_mine[part * slots + b:part * slots + b + 1, :] = jnp.sum(piece * piece, axis=0, keepdims=True)
    energy_copy = pltpu.make_async_remote_copy(
        src_ref=e_mine, dst_ref=e_sib, send_sem=e_send, recv_sem=e_recv, device_id=other, device_id_type=MESH)
    energy_copy.start()

    row = lax.broadcasted_iota(jnp.int32, (chans, 8, SPAN), 1)
    lane = lax.broadcasted_iota(jnp.int32, (chans, 8, SPAN), 2)

    def spread(x):
        return jnp.broadcast_to(x.astype(jnp.float32)[:, None, :], (chans, 8, SPAN))

    def block_at(at):
        lanes = pl.multiple_of(lax.rem(at, slots) * SPAN, SPAN)
        return spread(rec_all[at // slots, :, pl.ds(lanes, SPAN)])

    def shift_rows(now, after):
        y = jnp.where(lane >= row, now, after)
        for bit in (1, 2, 4):
            y = jnp.where((row & bit) > 0, pltpu.roll(y, SPAN - bit, 2), y)
        return y

    def build(pair, hankel):
        raw = [block_at(2 * pair + i) for i in (0, 1, 2, 2)]
        shifted = [shift_rows(raw[i], raw[i + 1]) for i in range(3)]
        for par in range(2):
            now, after = shifted[par], shifted[par + 1]
            for a in range(0, SPAN // 8, 2):
                both = []
                for d in (a, a + 1):
                    y = now
                    if d > 0:
                        y = pltpu.roll(jnp.where(lane >= 8 * d, now, after), SPAN - 8 * d, 2)
                    both.append(y)
                hankel[:, 8 * a:8 * a + 16, par * SPAN:(par + 1) * SPAN] = jnp.concatenate(both, axis=1).astype(jnp.bfloat16)

    def multiply(u, first, second, third):
        depth = chans * SPAN

        def straddle(left, right):
            return jnp.concatenate([left[:, :, SPAN:].reshape(depth, SPAN), right[:, :, :SPAN].reshape(depth, SPAN)], axis=1)

        sides = (first[...].reshape(depth, 2 * SPAN), straddle(first, second),
                 second[...].reshape(depth, 2 * SPAN), straddle(second, third))
        product = None
        for j in range(4):
            term = jnp.dot(lhs[j * rows:(j + 1) * rows, :], sides[j], preferred_element_type=jnp.float32)
            product = term if product is None else product + term
        for par in range(2):
            acc[2 * u + par] = product[:, par * SPAN:(par + 1) * SPAN]

    upper = jnp.where(z >= half, 1, 0)
    turn = (1 - upper) * (2 * n + 2) + upper * (n + 2)

    def pair_at(t):
        wrapped = jnp.where(t >= turn, 1, 0)
        return (1 - wrapped) * (turn - 1 - t) + wrapped * jnp.maximum(2 * n + 1 - (t - turn), 0)

    def chunk_at(t):
        wrapped = jnp.where(t >= turn, 1, 0)
        use = jnp.logical_and(t - wrapped * turn >= 2, jnp.logical_and(t >= 0, t < 2 * n + 2 + 2 * upper))
        return jnp.where(use, pair_at(t), -1)

    def sibling_copy(u):
        return pltpu.make_async_remote_copy(
            src_ref=acc.at[pl.ds(2 * u, 2)], dst_ref=sib.at[u],
            send_sem=sib_send.at[u], recv_sem=sib_recv.at[u], device_id=other, device_id_type=MESH)

    def result_copies(u, part):
        to = {"tm": u // 2, "chan": home}
        slot = part * 2 + u % 2
        return (
            pltpu.make_async_remote_copy(
                src_ref=codes.at[u], dst_ref=codes_in.at[part, pl.ds(2 * (u % 2), 2)], send_sem=code_send.at[u],
                recv_sem=code_recv.at[slot], device_id=to, device_id_type=MESH),
            pltpu.make_async_remote_copy(
                src_ref=scales.at[u], dst_ref=scales_in.at[part, pl.ds(2 * (u % 2), 2)], send_sem=scale_send.at[u],
                recv_sem=scale_recv.at[slot], device_id=to, device_id_type=MESH),
        )

    def hand_over(u):
        @pl.when(jnp.logical_and(jnp.logical_and(u >= 0, u < 2 * n), lax.rem(u + 2, 2) != core))
        def _():
            sibling_copy(u).start()

    def finish(u):
        @pl.when(jnp.logical_and(jnp.logical_and(u >= 0, u < 2 * n), lax.rem(u + 2, 2) == core))
        def _():
            sibling_copy(u).wait_recv()
            keep = jnp.logical_and(u // 2 == z, core == home)
            for b in range(2):
                total = acc[2 * u + b] + sib[u, b]
                top = jnp.maximum(jnp.max(jnp.abs(total), axis=0, keepdims=True), 1e-37)
                coded = jnp.round((total * (1.0 / top)) * CODES).astype(jnp.int32).astype(jnp.int16)
                scale = jnp.broadcast_to(top * (1.0 / CODES), (8, SPAN))

                @pl.when(keep)
                def _():
                    codes_in[own_part, 2 * core + b] = coded
                    scales_in[own_part, 2 * core + b] = scale

                @pl.when(jnp.logical_not(keep))
                def _():
                    codes[u, b] = coded
                    scales[u, b] = scale

            @pl.when(jnp.logical_not(keep))
            def _():
                for copy in result_copies(u, own_part):
                    copy.start()

    build(pair_at(0), ring[0])

    def step(i, _):
        for r in range(4):
            t = 4 * i + r
            u = chunk_at(t)
            following = pair_at(jnp.minimum(t + 1, 2 * n + 3))

            @pl.when(u >= 0)
            def _():
                build(following, ring[(r + 1) % 4])
                multiply(u, ring[r], ring[(r + 3) % 4], ring[(r + 2) % 4])

            @pl.when(jnp.logical_and(u < 0, t + 1 < 2 * n + 2 + 2 * upper))
            def _():
                build(following, ring[(r + 1) % 4])

            hand_over(u)
            finish(chunk_at(t - 1))
        return 0

    lax.fori_loop(0, (2 * n + 4) // 4, step, 0)
    finish(chunk_at(2 * n + 3))

    energy_copy.wait()
    e = e_mine[...] + e_sib[...]
    i0 = lax.broadcasted_iota(jnp.int32, (SPAN, SPAN), 0)
    i1 = lax.broadcasted_iota(jnp.int32, (SPAN, SPAN), 1)
    dot = functools.partial(jnp.dot, preferred_element_type=jnp.float32, precision=lax.Precision.HIGHEST)
    tails = dot(e, jnp.where(i0 >= i1, 1.0, 0.0))
    heads = dot(e, jnp.where(i0 < i1, 1.0, 0.0))
    sums = jnp.sum(e, axis=1, keepdims=True)
    for b in range(slots):
        energy = tails[b:b + 1] + heads[b + 4:b + 5] + sums[b + 1:b + 2] + sums[b + 2:b + 3] + sums[b + 3:b + 4]
        e_mine[b:b + 1, :] = lax.rsqrt(energy / (2 * chans * 4 * SPAN) + 1e-05)

    def arrival(i, _):
        part, from_core = i // 2, i % 2
        source = core * half + part

        @pl.when(jnp.logical_not(jnp.logical_and(source == z, from_core == core)))
        def _():
            for copy in result_copies(from_core, part):
                copy.wait_recv()

        return 0

    lax.fori_loop(0, n, arrival, 0)

    for slot in range(slots):
        at = span_ref[0, slot]
        block = jnp.maximum(at, 0)
        inverse = jnp.where(at >= 0, e_mine[pl.ds(block, 1), :], 0.0)
        for part in range(half):
            values = codes_in[part, block].astype(jnp.int32).astype(jnp.float32)
            scale = scales_in[part, block, 0:1] * inverse
            out_ref[part * rows:(part + 1) * rows, slot * SPAN:(slot + 1) * SPAN] = values * scale

    def drain(u, _):
        mine = u % 2 == core

        @pl.when(jnp.logical_not(mine))
        def _():
            sibling_copy(u).wait_send()

        @pl.when(jnp.logical_and(mine, jnp.logical_not(jnp.logical_and(u // 2 == z, core == home))))
        def _():
            for copy in result_copies(u, own_part):
                copy.wait_send()

        return 0

    lax.fori_loop(0, 2 * n, drain, 0)
    lax.fori_loop(1, n, lambda i, _: (record_copy(i).wait_send(), 0)[1], 0)


def local(n, record, templates, span_list):
    _, rows, chans, _ = templates.shape
    slots = span_list.shape[1]
    vmem = pl.BlockSpec(memory_space=pltpu.VMEM)
    dma = pltpu.SemaphoreType.DMA
    return pl.pallas_call(
        functools.partial(kernel, n, rows, chans, slots),
        out_shape=jax.ShapeDtypeStruct((rows * n // 2, slots * SPAN), jnp.float32),
        in_specs=[pl.BlockSpec(memory_space=pltpu.SMEM), vmem, pl.BlockSpec(memory_space=pltpu.HBM)],
        out_specs=vmem,
        scratch_shapes=[
            pltpu.VMEM(templates.shape[1:], jnp.bfloat16),
            pltpu.VMEM((4 * rows, chans * SPAN), jnp.bfloat16),
            pltpu.VMEM((n + 2, chans, record.shape[1]), jnp.bfloat16),
            pltpu.VMEM((chans, SPAN, 2 * SPAN), jnp.bfloat16),
            pltpu.VMEM((chans, SPAN, 2 * SPAN), jnp.bfloat16),
            pltpu.VMEM((chans, SPAN, 2 * SPAN), jnp.bfloat16),
            pltpu.VMEM((chans, SPAN, 2 * SPAN), jnp.bfloat16),
            pltpu.VMEM((4 * n, rows, SPAN), jnp.float32),
            pltpu.VMEM((2 * n, 2, rows, SPAN), jnp.float32),
            pltpu.VMEM((2 * n, 2, rows, SPAN), jnp.int16),
            pltpu.VMEM((2 * n, 2, 8, SPAN), jnp.float32),
            pltpu.VMEM((n // 2, 4, rows, SPAN), jnp.int16),
            pltpu.VMEM((n // 2, 4, 8, SPAN), jnp.float32),
            pltpu.VMEM((8, SPAN), jnp.float32),
            pltpu.VMEM((8, SPAN), jnp.float32),
            dma((n,)), dma((n,)), dma((2 * n,)), dma((2 * n,)), dma((2 * n,)), dma((n,)), dma((2 * n,)), dma((n,)),
            dma, dma, dma,
        ],
        compiler_params=pltpu.CompilerParams(collective_id=0, has_side_effects=True, vmem_limit_bytes=62 * 2**20),
    )(span_list, record, templates)


def solution(mesh):
    in_specs = (P("chan", ("grp", "tm")), P("tmpl", "tm", "chan", None), P(("grp", "tm"), None))
    out_specs = P(("tmpl", "chan"), ("grp", "tm"))
    return jax.shard_map(functools.partial(local, mesh.shape["tm"]), mesh=mesh, in_specs=in_specs, out_specs=out_specs, check_vma=False)
```

```python
import functools

import jax
import jax.numpy as jnp
from jax import lax
from jax.experimental import pallas as pl
from jax.experimental.pallas import tpu as pltpu
from jax.sharding import PartitionSpec as P

SPAN = 128
CODES = 32767.0
MESH = pl.DeviceIdType.MESH


def kernel(n, rows, chans, slots, span_ref, rec_ref, tmpl_ref, out_ref, tmpl, lhs, rec_all, ring_a, ring_b, ring_c, ring_d, acc, sib, codes, scales,
           codes_in, scales_in, e_mine, e_sib, rec_send, rec_recv, sib_send, sib_recv, code_send, code_recv,
           scale_send, scale_recv, e_send, e_recv, tmpl_sem):
    z = lax.axis_index("tm")
    core = lax.axis_index("chan")
    half = n // 2
    home = z // half
    own_part = z % half
    other = {"tm": z, "chan": 1 - core}
    ring = (ring_a, ring_b, ring_c, ring_d)

    tmpl_copy = pltpu.make_async_copy(tmpl_ref.at[0], tmpl, tmpl_sem)
    tmpl_copy.start()
    barrier = pltpu.get_barrier_semaphore()

    def greet(i, _):
        peer = lax.rem(z + i // 2, n)
        to = lax.rem(core + i % 2, 2)
        pl.semaphore_signal(barrier, inc=1, device_id={"tm": peer, "chan": to}, device_id_type=MESH)
        return 0

    lax.fori_loop(1, 2 * n, greet, 0)
    rec_all[z] = rec_ref[...]
    rec_all[n] = jnp.zeros_like(rec_ref)
    rec_all[n + 1] = jnp.zeros_like(rec_ref)
    tmpl_copy.wait()
    group = 16 if rows % 16 == 0 else 8

    def arrange(g, _):
        for j in range(4):
            turned = jnp.swapaxes(tmpl[pl.ds(g * group, group), :, j * SPAN:(j + 1) * SPAN], 0, 1)
            at = pl.multiple_of(j * rows + g * group, group)
            for c in range(chans):
                lhs[pl.ds(at, group), c * SPAN:(c + 1) * SPAN] = turned[c]
        return 0

    pl.semaphore_wait(barrier, 2 * n - 1)

    def record_copy(i):
        peer = lax.rem(z + i, n)
        return pltpu.make_async_remote_copy(
            src_ref=rec_ref, dst_ref=rec_all.at[z], send_sem=rec_send.at[peer], recv_sem=rec_recv.at[z],
            device_id={"tm": peer, "chan": core}, device_id_type=MESH)

    def record_arrival(i):
        peer = lax.rem(z + i, n)
        return pltpu.make_async_remote_copy(
            src_ref=rec_ref, dst_ref=rec_all.at[peer], send_sem=rec_send.at[peer], recv_sem=rec_recv.at[peer],
            device_id={"tm": peer, "chan": core}, device_id_type=MESH)

    lax.fori_loop(1, n, lambda i, _: (record_copy(i).start(), 0)[1], 0)

    lax.fori_loop(0, rows // group, arrange, 0)

    row = lax.broadcasted_iota(jnp.int32, (chans, 8, SPAN), 1)
    lane = lax.broadcasted_iota(jnp.int32, (chans, 8, SPAN), 2)

    def spread(x):
        return jnp.broadcast_to(x.astype(jnp.float32)[:, None, :], (chans, 8, SPAN))

    def block_at(at):
        lanes = pl.multiple_of(lax.rem(at, slots) * SPAN, SPAN)
        return spread(rec_all[at // slots, :, pl.ds(lanes, SPAN)])

    def shift_rows(now, after):
        y = jnp.where(lane >= row, now, after)
        for bit in (1, 2, 4):
            y = jnp.where((row & bit) > 0, pltpu.roll(y, SPAN - bit, 2), y)
        return y

    def build(pair, hankel, pars=(0, 1)):
        raw = [block_at(2 * pair + i) for i in (0, 1, 2, 2)]
        shifted = [shift_rows(raw[i], raw[i + 1]) for i in range(3)]
        for par in pars:
            now, after = shifted[par], shifted[par + 1]
            for a in range(0, SPAN // 8, 2):
                both = []
                for d in (a, a + 1):
                    y = now
                    if d > 0:
                        y = pltpu.roll(jnp.where(lane >= 8 * d, now, after), SPAN - 8 * d, 2)
                    both.append(y)
                hankel[:, 8 * a:8 * a + 16, par * SPAN:(par + 1) * SPAN] = jnp.concatenate(both, axis=1).astype(jnp.bfloat16)

    def multiply(u, first, second, third):
        depth = chans * SPAN

        def straddle(left, right):
            return jnp.concatenate([left[:, :, SPAN:].reshape(depth, SPAN), right[:, :, :SPAN].reshape(depth, SPAN)], axis=1)

        sides = (first[...].reshape(depth, 2 * SPAN), straddle(first, second),
                 second[...].reshape(depth, 2 * SPAN), straddle(second, third))
        product = None
        for j in range(4):
            term = jnp.dot(lhs[j * rows:(j + 1) * rows, :], sides[j], preferred_element_type=jnp.float32)
            product = term if product is None else product + term
        for par in range(2):
            acc[2 * u + par] = product[:, par * SPAN:(par + 1) * SPAN]

    upper = jnp.where(z >= half, 1, 0)
    turn = (1 - upper) * (2 * n + 2) + upper * (n + 2)

    def pair_at(t):
        wrapped = jnp.where(t >= turn, 1, 0)
        return (1 - wrapped) * (turn - 1 - t) + wrapped * jnp.maximum(2 * n + 1 - (t - turn), 0)

    def chunk_at(t):
        wrapped = jnp.where(t >= turn, 1, 0)
        use = jnp.logical_and(t - wrapped * turn >= 2, jnp.logical_and(t >= 0, t < 2 * n + 2 + 2 * upper))
        return jnp.where(use, pair_at(t), -1)

    def sibling_copy(u):
        return pltpu.make_async_remote_copy(
            src_ref=acc.at[2 * u + 1 - core], dst_ref=sib.at[u],
            send_sem=sib_send.at[u], recv_sem=sib_recv.at[u], device_id=other, device_id_type=MESH)

    def result_copies(u, part, from_core):
        to = {"tm": u // 2, "chan": home}
        block = 2 * (u % 2) + from_core
        slot = part * 4 + block
        return (
            pltpu.make_async_remote_copy(
                src_ref=codes.at[u], dst_ref=codes_in.at[part, block], send_sem=code_send.at[u],
                recv_sem=code_recv.at[slot], device_id=to, device_id_type=MESH),
            pltpu.make_async_remote_copy(
                src_ref=scales.at[u], dst_ref=scales_in.at[part, block], send_sem=scale_send.at[u],
                recv_sem=scale_recv.at[slot], device_id=to, device_id_type=MESH),
        )

    def finish(u, when=True):
        @pl.when(jnp.logical_and(u >= 0, when))
        def _():
            sibling_copy(u).wait_recv()
            keep = jnp.logical_and(u // 2 == z, core == home)
            total = acc[2 * u + core] + sib[u]
            top = jnp.maximum(jnp.max(jnp.abs(total), axis=0, keepdims=True), 1e-37)
            coded = jnp.round((total * (1.0 / top)) * CODES).astype(jnp.int32).astype(jnp.int16)
            scale = jnp.broadcast_to(top * (1.0 / CODES), (8, SPAN))

            @pl.when(keep)
            def _():
                codes_in[own_part, 2 * (u % 2) + core] = coded
                scales_in[own_part, 2 * (u % 2) + core] = scale

            @pl.when(jnp.logical_not(keep))
            def _():
                codes[u] = coded
                scales[u] = scale
                for copy in result_copies(u, own_part, core):
                    copy.start()

    def begin():
        build(pair_at(0), ring[0], (0,))
        build(pair_at(1), ring[1])

    pl.when(upper == 0)(begin)
    lax.fori_loop(1, n, lambda i, _: (record_arrival(i).wait_recv(), 0)[1], 0)
    for part in range(2):
        for b in range(slots):
            piece = rec_all[z + part, :, b * SPAN:(b + 1) * SPAN].astype(jnp.float32)
            e_mine[part * slots + b:part * slots + b + 1, :] = jnp.sum(piece * piece, axis=0, keepdims=True)
    energy_copy = pltpu.make_async_remote_copy(
        src_ref=e_mine, dst_ref=e_sib, send_sem=e_send, recv_sem=e_recv, device_id=other, device_id_type=MESH)
    energy_copy.start()

    pl.when(upper == 1)(begin)


    def step(i, _):
        for r in range(4):
            t = 4 * i + r
            u = chunk_at(t)
            following = pair_at(jnp.minimum(t + 1, 2 * n + 3))

            @pl.when(u >= 0)
            def _():
                build(following, ring[(r + 1) % 4])
                multiply(u, ring[r], ring[(r + 3) % 4], ring[(r + 2) % 4])

            @pl.when(jnp.logical_and(jnp.logical_and(u < 0, t > 0), t + 1 < 2 * n + 2 + 2 * upper))
            def _():
                build(following, ring[(r + 1) % 4])

            @pl.when(u >= 0)
            def _():
                sibling_copy(u).start()

            if r == 2:
                finish(chunk_at(t - 1))
            elif r == 3:
                finish(chunk_at(t - 1))
            else:
                finish(chunk_at(t - 1))
        return 0

    lax.fori_loop(0, (2 * n + 4) // 4, step, 0)
    finish(chunk_at(2 * n + 3))

    energy_copy.wait()
    e = e_mine[...] + e_sib[...]
    i0 = lax.broadcasted_iota(jnp.int32, (SPAN, SPAN), 0)
    i1 = lax.broadcasted_iota(jnp.int32, (SPAN, SPAN), 1)
    dot = functools.partial(jnp.dot, preferred_element_type=jnp.float32, precision=lax.Precision.HIGHEST)
    tails = dot(e, jnp.where(i0 >= i1, 1.0, 0.0))
    heads = dot(e, jnp.where(i0 < i1, 1.0, 0.0))
    sums = jnp.sum(e, axis=1, keepdims=True)
    for b in range(slots):
        energy = tails[b:b + 1] + heads[b + 4:b + 5] + sums[b + 1:b + 2] + sums[b + 2:b + 3] + sums[b + 3:b + 4]
        e_mine[b:b + 1, :] = lax.rsqrt(energy / (2 * chans * 4 * SPAN) + 1e-05)

    def arrival(i, _):
        part, block = i // 4, i % 4
        from_core = block % 2
        source = core * half + part

        @pl.when(jnp.logical_not(jnp.logical_and(source == z, from_core == core)))
        def _():
            for copy in result_copies(block // 2, part, from_core):
                copy.wait_recv()

        return 0

    lax.fori_loop(0, 2 * n, arrival, 0)

    for slot in range(slots):
        at = span_ref[0, slot]
        block = jnp.maximum(at, 0)
        inverse = jnp.where(at >= 0, e_mine[pl.ds(block, 1), :], 0.0)
        for part in range(half):
            values = codes_in[part, block].astype(jnp.int32).astype(jnp.float32)
            scale = scales_in[part, block, 0:1] * inverse
            out_ref[part * rows:(part + 1) * rows, slot * SPAN:(slot + 1) * SPAN] = values * scale

    def drain(u, _):
        sibling_copy(u).wait_send()

        @pl.when(jnp.logical_not(jnp.logical_and(u // 2 == z, core == home)))
        def _():
            for copy in result_copies(u, own_part, core):
                copy.wait_send()

        return 0

    lax.fori_loop(0, 2 * n, drain, 0)
    lax.fori_loop(1, n, lambda i, _: (record_copy(i).wait_send(), 0)[1], 0)


def local(n, record, templates, span_list):
    _, rows, chans, _ = templates.shape
    slots = span_list.shape[1]
    vmem = pl.BlockSpec(memory_space=pltpu.VMEM)
    dma = pltpu.SemaphoreType.DMA
    return pl.pallas_call(
        functools.partial(kernel, n, rows, chans, slots),
        out_shape=jax.ShapeDtypeStruct((rows * n // 2, slots * SPAN), jnp.float32),
        in_specs=[pl.BlockSpec(memory_space=pltpu.SMEM), vmem, pl.BlockSpec(memory_space=pltpu.HBM)],
        out_specs=vmem,
        scratch_shapes=[
            pltpu.VMEM(templates.shape[1:], jnp.bfloat16),
            pltpu.VMEM((4 * rows, chans * SPAN), jnp.bfloat16),
            pltpu.VMEM((n + 2, chans, record.shape[1]), jnp.bfloat16),
            pltpu.VMEM((chans, SPAN, 2 * SPAN), jnp.bfloat16),
            pltpu.VMEM((chans, SPAN, 2 * SPAN), jnp.bfloat16),
            pltpu.VMEM((chans, SPAN, 2 * SPAN), jnp.bfloat16),
            pltpu.VMEM((chans, SPAN, 2 * SPAN), jnp.bfloat16),
            pltpu.VMEM((4 * n, rows, SPAN), jnp.float32),
            pltpu.VMEM((2 * n, rows, SPAN), jnp.float32),
            pltpu.VMEM((2 * n, rows, SPAN), jnp.int16),
            pltpu.VMEM((2 * n, 8, SPAN), jnp.float32),
            pltpu.VMEM((n // 2, 4, rows, SPAN), jnp.int16),
            pltpu.VMEM((n // 2, 4, 8, SPAN), jnp.float32),
            pltpu.VMEM((8, SPAN), jnp.float32),
            pltpu.VMEM((8, SPAN), jnp.float32),
            dma((n,)), dma((n,)), dma((2 * n,)), dma((2 * n,)), dma((2 * n,)), dma((2 * n,)), dma((2 * n,)), dma((2 * n,)),
            dma, dma, dma,
        ],
        compiler_params=pltpu.CompilerParams(collective_id=0, has_side_effects=True, vmem_limit_bytes=62 * 2**20),
    )(span_list, record, templates)


def solution(mesh):
    in_specs = (P("chan", ("grp", "tm")), P("tmpl", "tm", "chan", None), P(("grp", "tm"), None))
    out_specs = P(("tmpl", "chan"), ("grp", "tm"))
    return jax.shard_map(functools.partial(local, mesh.shape["tm"]), mesh=mesh, in_specs=in_specs, out_specs=out_specs, check_vma=False)
```

```python
import functools

import jax
import jax.numpy as jnp
from jax import lax
from jax.experimental import pallas as pl
from jax.experimental.pallas import tpu as pltpu
from jax.sharding import PartitionSpec as P

SPAN = 128
CODES = 32767.0
MESH = pl.DeviceIdType.MESH


def kernel(n, rows, chans, slots, span_ref, rec_ref, tmpl_ref, out_ref, tmpl, lhs, rec_all, ring_a, ring_b, ring_c, ring_d, acc, sib, codes, scales,
           codes_in, scales_in, e_mine, e_sib, rec_send, rec_recv, sib_send, sib_recv, code_send, code_recv,
           scale_send, scale_recv, e_send, e_recv, tmpl_sem):
    z = lax.axis_index("tm")
    core = lax.axis_index("chan")
    half = n // 2
    home = z // half
    own_part = z % half
    other = {"tm": z, "chan": 1 - core}
    ring = (ring_a, ring_b, ring_c, ring_d)

    tmpl_copy = pltpu.make_async_copy(tmpl_ref.at[0], tmpl, tmpl_sem)
    tmpl_copy.start()
    barrier = pltpu.get_barrier_semaphore()

    def greet(i, _):
        peer = lax.rem(z + i // 2, n)
        to = lax.rem(core + i % 2, 2)
        pl.semaphore_signal(barrier, inc=1, device_id={"tm": peer, "chan": to}, device_id_type=MESH)
        return 0

    lax.fori_loop(1, 2 * n, greet, 0)
    rec_all[z] = rec_ref[...]
    rec_all[n] = jnp.zeros_like(rec_ref)
    rec_all[n + 1] = jnp.zeros_like(rec_ref)
    tmpl_copy.wait()
    group = 16 if rows % 16 == 0 else 8

    def arrange(g, _):
        for j in range(4):
            turned = jnp.swapaxes(tmpl[pl.ds(g * group, group), :, j * SPAN:(j + 1) * SPAN], 0, 1)
            at = pl.multiple_of(j * rows + g * group, group)
            for c in range(chans):
                lhs[pl.ds(at, group), c * SPAN:(c + 1) * SPAN] = turned[c]
        return 0

    lax.fori_loop(0, rows // group, arrange, 0)
    pl.semaphore_wait(barrier, 2 * n - 1)

    def record_copy(i):
        peer = lax.rem(z + i, n)
        return pltpu.make_async_remote_copy(
            src_ref=rec_ref, dst_ref=rec_all.at[z], send_sem=rec_send.at[peer], recv_sem=rec_recv.at[z],
            device_id={"tm": peer, "chan": core}, device_id_type=MESH)

    def record_arrival(i):
        peer = lax.rem(z + i, n)
        return pltpu.make_async_remote_copy(
            src_ref=rec_ref, dst_ref=rec_all.at[peer], send_sem=rec_send.at[peer], recv_sem=rec_recv.at[peer],
            device_id={"tm": peer, "chan": core}, device_id_type=MESH)

    lax.fori_loop(1, n, lambda i, _: (record_copy(i).start(), 0)[1], 0)


    row = lax.broadcasted_iota(jnp.int32, (chans, 8, SPAN), 1)
    lane = lax.broadcasted_iota(jnp.int32, (chans, 8, SPAN), 2)

    def spread(x):
        return jnp.broadcast_to(x.astype(jnp.float32)[:, None, :], (chans, 8, SPAN))

    def block_at(at):
        lanes = pl.multiple_of(lax.rem(at, slots) * SPAN, SPAN)
        return spread(rec_all[at // slots, :, pl.ds(lanes, SPAN)])

    def shift_rows(now, after):
        y = jnp.where(lane >= row, now, after)
        for bit in (1, 2, 4):
            y = jnp.where((row & bit) > 0, pltpu.roll(y, SPAN - bit, 2), y)
        return y

    def build(pair, hankel, pars=(0, 1)):
        raw = [block_at(2 * pair + i) for i in (0, 1, 2, 2)]
        shifted = [shift_rows(raw[i], raw[i + 1]) for i in range(3)]
        for par in pars:
            now, after = shifted[par], shifted[par + 1]
            for a in range(0, SPAN // 8, 2):
                both = []
                for d in (a, a + 1):
                    y = now
                    if d > 0:
                        y = pltpu.roll(jnp.where(lane >= 8 * d, now, after), SPAN - 8 * d, 2)
                    both.append(y)
                hankel[:, 8 * a:8 * a + 16, par * SPAN:(par + 1) * SPAN] = jnp.concatenate(both, axis=1).astype(jnp.bfloat16)

    def multiply(u, first, second, third):
        depth = chans * SPAN

        def straddle(left, right):
            return jnp.concatenate([left[:, :, SPAN:].reshape(depth, SPAN), right[:, :, :SPAN].reshape(depth, SPAN)], axis=1)

        sides = (first[...].reshape(depth, 2 * SPAN), straddle(first, second),
                 second[...].reshape(depth, 2 * SPAN), straddle(second, third))
        product = None
        for j in range(4):
            term = jnp.dot(lhs[j * rows:(j + 1) * rows, :], sides[j], preferred_element_type=jnp.float32)
            product = term if product is None else product + term
        for par in range(2):
            acc[2 * u + par] = product[:, par * SPAN:(par + 1) * SPAN]

    upper = jnp.where(z >= half, 1, 0)
    turn = (1 - upper) * (2 * n + 2) + upper * (n + 2)

    def pair_at(t):
        wrapped = jnp.where(t >= turn, 1, 0)
        return (1 - wrapped) * (turn - 1 - t) + wrapped * jnp.maximum(2 * n + 1 - (t - turn), 0)

    def chunk_at(t):
        wrapped = jnp.where(t >= turn, 1, 0)
        use = jnp.logical_and(t - wrapped * turn >= 2, jnp.logical_and(t >= 0, t < 2 * n + 2 + 2 * upper))
        return jnp.where(use, pair_at(t), -1)

    def sibling_copy(u):
        return pltpu.make_async_remote_copy(
            src_ref=acc.at[2 * u + 1 - core], dst_ref=sib.at[u],
            send_sem=sib_send.at[u], recv_sem=sib_recv.at[u], device_id=other, device_id_type=MESH)

    def result_copies(u, part, from_core):
        to = {"tm": u // 2, "chan": home}
        block = 2 * (u % 2) + from_core
        slot = part * 4 + block
        return (
            pltpu.make_async_remote_copy(
                src_ref=codes.at[u], dst_ref=codes_in.at[part, block], send_sem=code_send.at[u],
                recv_sem=code_recv.at[slot], device_id=to, device_id_type=MESH),
            pltpu.make_async_remote_copy(
                src_ref=scales.at[u], dst_ref=scales_in.at[part, block], send_sem=scale_send.at[u],
                recv_sem=scale_recv.at[slot], device_id=to, device_id_type=MESH),
        )

    def finish(u, when=True):
        @pl.when(jnp.logical_and(u >= 0, when))
        def _():
            sibling_copy(u).wait_recv()
            keep = jnp.logical_and(u // 2 == z, core == home)
            total = acc[2 * u + core] + sib[u]
            top = jnp.maximum(jnp.max(jnp.abs(total), axis=0, keepdims=True), 1e-37)
            coded = jnp.round((total * (1.0 / top)) * CODES).astype(jnp.int32).astype(jnp.int16)
            scale = jnp.broadcast_to(top * (1.0 / CODES), (8, SPAN))

            @pl.when(keep)
            def _():
                codes_in[own_part, 2 * (u % 2) + core] = coded
                scales_in[own_part, 2 * (u % 2) + core] = scale

            @pl.when(jnp.logical_not(keep))
            def _():
                codes[u] = coded
                scales[u] = scale
                for copy in result_copies(u, own_part, core):
                    copy.start()

    def begin():
        build(pair_at(0), ring[0], (0,))
        build(pair_at(1), ring[1])

    pl.when(upper == 0)(begin)
    lax.fori_loop(1, n, lambda i, _: (record_arrival(i).wait_recv(), 0)[1], 0)
    for part in range(2):
        for b in range(slots):
            piece = rec_all[z + part, :, b * SPAN:(b + 1) * SPAN].astype(jnp.float32)
            e_mine[part * slots + b:part * slots + b + 1, :] = jnp.sum(piece * piece, axis=0, keepdims=True)
    energy_copy = pltpu.make_async_remote_copy(
        src_ref=e_mine, dst_ref=e_sib, send_sem=e_send, recv_sem=e_recv, device_id=other, device_id_type=MESH)
    energy_copy.start()

    pl.when(upper == 1)(begin)


    def step(i, _):
        for r in range(4):
            t = 4 * i + r
            u = chunk_at(t)
            following = pair_at(jnp.minimum(t + 1, 2 * n + 3))

            @pl.when(u >= 0)
            def _():
                build(following, ring[(r + 1) % 4])
                multiply(u, ring[r], ring[(r + 3) % 4], ring[(r + 2) % 4])

            @pl.when(jnp.logical_and(jnp.logical_and(u < 0, t > 0), t + 1 < 2 * n + 2 + 2 * upper))
            def _():
                build(following, ring[(r + 1) % 4])

            @pl.when(u >= 0)
            def _():
                sibling_copy(u).start()

            if r == 2:
                finish(chunk_at(t - 1))
            elif r == 3:
                finish(chunk_at(t - 1))
            else:
                finish(chunk_at(t - 1))
        return 0

    lax.fori_loop(0, (2 * n + 4) // 4, step, 0)
    finish(chunk_at(2 * n + 3))

    energy_copy.wait()
    e = e_mine[...] + e_sib[...]
    i0 = lax.broadcasted_iota(jnp.int32, (SPAN, SPAN), 0)
    i1 = lax.broadcasted_iota(jnp.int32, (SPAN, SPAN), 1)
    dot = functools.partial(jnp.dot, preferred_element_type=jnp.float32, precision=lax.Precision.HIGHEST)
    tails = dot(e, jnp.where(i0 >= i1, 1.0, 0.0))
    heads = dot(e, jnp.where(i0 < i1, 1.0, 0.0))
    sums = jnp.sum(e, axis=1, keepdims=True)
    for b in range(slots):
        energy = tails[b:b + 1] + heads[b + 4:b + 5] + sums[b + 1:b + 2] + sums[b + 2:b + 3] + sums[b + 3:b + 4]
        e_mine[b:b + 1, :] = lax.rsqrt(energy / (2 * chans * 4 * SPAN) + 1e-05)

    def arrival(i, _):
        part, block = i // 4, i % 4
        from_core = block % 2
        source = core * half + part

        @pl.when(jnp.logical_not(jnp.logical_and(source == z, from_core == core)))
        def _():
            for copy in result_copies(block // 2, part, from_core):
                copy.wait_recv()

        return 0

    lax.fori_loop(0, 2 * n, arrival, 0)

    for slot in range(slots):
        at = span_ref[0, slot]
        block = jnp.maximum(at, 0)
        inverse = jnp.where(at >= 0, e_mine[pl.ds(block, 1), :], 0.0)
        for part in range(half):
            values = codes_in[part, block].astype(jnp.int32).astype(jnp.float32)
            scale = scales_in[part, block, 0:1] * inverse
            out_ref[part * rows:(part + 1) * rows, slot * SPAN:(slot + 1) * SPAN] = values * scale

    def drain(u, _):
        sibling_copy(u).wait_send()

        @pl.when(jnp.logical_not(jnp.logical_and(u // 2 == z, core == home)))
        def _():
            for copy in result_copies(u, own_part, core):
                copy.wait_send()

        return 0

    lax.fori_loop(0, 2 * n, drain, 0)
    lax.fori_loop(1, n, lambda i, _: (record_copy(i).wait_send(), 0)[1], 0)


def local(n, record, templates, span_list):
    _, rows, chans, _ = templates.shape
    slots = span_list.shape[1]
    vmem = pl.BlockSpec(memory_space=pltpu.VMEM)
    dma = pltpu.SemaphoreType.DMA
    return pl.pallas_call(
        functools.partial(kernel, n, rows, chans, slots),
        out_shape=jax.ShapeDtypeStruct((rows * n // 2, slots * SPAN), jnp.float32),
        in_specs=[pl.BlockSpec(memory_space=pltpu.SMEM), vmem, pl.BlockSpec(memory_space=pltpu.HBM)],
        out_specs=vmem,
        scratch_shapes=[
            pltpu.VMEM(templates.shape[1:], jnp.bfloat16),
            pltpu.VMEM((4 * rows, chans * SPAN), jnp.bfloat16),
            pltpu.VMEM((n + 2, chans, record.shape[1]), jnp.bfloat16),
            pltpu.VMEM((chans, SPAN, 2 * SPAN), jnp.bfloat16),
            pltpu.VMEM((chans, SPAN, 2 * SPAN), jnp.bfloat16),
            pltpu.VMEM((chans, SPAN, 2 * SPAN), jnp.bfloat16),
            pltpu.VMEM((chans, SPAN, 2 * SPAN), jnp.bfloat16),
            pltpu.VMEM((4 * n, rows, SPAN), jnp.float32),
            pltpu.VMEM((2 * n, rows, SPAN), jnp.float32),
            pltpu.VMEM((2 * n, rows, SPAN), jnp.int16),
            pltpu.VMEM((2 * n, 8, SPAN), jnp.float32),
            pltpu.VMEM((n // 2, 4, rows, SPAN), jnp.int16),
            pltpu.VMEM((n // 2, 4, 8, SPAN), jnp.float32),
            pltpu.VMEM((8, SPAN), jnp.float32),
            pltpu.VMEM((8, SPAN), jnp.float32),
            dma((n,)), dma((n,)), dma((2 * n,)), dma((2 * n,)), dma((2 * n,)), dma((2 * n,)), dma((2 * n,)), dma((2 * n,)),
            dma, dma, dma,
        ],
        compiler_params=pltpu.CompilerParams(collective_id=0, has_side_effects=True, vmem_limit_bytes=62 * 2**20),
    )(span_list, record, templates)


def solution(mesh):
    in_specs = (P("chan", ("grp", "tm")), P("tmpl", "tm", "chan", None), P(("grp", "tm"), None))
    out_specs = P(("tmpl", "chan"), ("grp", "tm"))
    return jax.shard_map(functools.partial(local, mesh.shape["tm"]), mesh=mesh, in_specs=in_specs, out_specs=out_specs, check_vma=False)
```
